32 devices in a mesh: chain: 16 (over z, x, core), rep: 2 (over y).
Axes of the slice: x: 2, y: 2, z: 4, core: 2. Of those that a mesh axis runs over, the one named last changes fastest.
Arguments:
- spins: bfloat16 [24576, 256], P('chain'), may hold values from -1 to 1, as said below
- energies: bfloat16 [24576], P('chain'), may hold values from -150 to -70
- counts: int32 [16], P('chain'), may hold values from 1 to 1536, 12288 in all
- accepted: int32 [16, 1536], P('chain'), may hold values from 0 to 1535, each once within a row
- hidden_bias: bfloat16 [4096], P('rep'), may hold values from -3 to 3
- weights: bfloat16 [256, 4096], P(None, 'rep'), may hold values from -0.375 to 0.375
Outputs:
- update_visible: float32 [256], P('rep')
- update_hidden: float32 [4096], P('rep')
- update_weights: float32 [256, 4096], P('chain', 'rep')
The draws below stay inside these ranges and needn't reach their ends.
Inputs may be any that keep to these rules, and one draw needn't show every extreme that they name: `spins`: every entry is -1 or 1. The counts sum to 12288; at least one index of chain has 1536. Each row is a permutation of the slot numbers; its first counts entries name that index's accepted slots.
All inputs are finite; a program needn't handle non-finite values. No bound on the sum of `counts` on one device may be relied on, other than what follows from the above.
Results may differ from the reference program's by a relative error of at most 0.02.
Values may be sent and summed in bfloat16 or wider, within the bound.
A program may use at most 64 MiB of HBM per device.

```python
import math
import jax
import jax.numpy as jnp
import numpy as np
from jax import lax

N_SITES = 256
HIDDEN_SIZE = 4096
KEEP_DEV = 768
ITERS = 3
SLOTS_DEV = 1536
SLOTS_ALL = 24576
TOTAL = 12288
N_CHAIN = 16


def draw_spins(key, part):
    coin_flips = jax.random.randint(key, (SLOTS_ALL, N_SITES), 0, 2)
    return (2 * coin_flips - 1).astype(jnp.bfloat16)


def steps_of(stream_key, extent, split, smallest, largest):
    def one(dim, parts):
        steps = jax.random.uniform(jax.random.fold_in(jax.random.fold_in(stream_key, 6), dim), (parts,), jnp.float32, smallest / len(split), largest / len(split))
        return jnp.repeat(jnp.exp(steps), extent[dim] // parts).reshape((-1,) + (1,) * (len(extent) - dim - 1))

    level = one(*split[0])
    for cut in split[1:]:
        level = level * one(*cut)
    return level


def length_profile(amount, total, bound, slope):
    loads = [(1 << 20) // math.isqrt(grade ** slope) + 1 for grade in range(2, amount + 1)]
    rest, holding = total - bound - (amount - 1), [1] * (amount - 1)
    while rest > 0:
        movable = [i for i in range(amount - 1) if holding[i] < bound]
        whole, remaining = sum([loads[i] for i in movable]), rest
        for i in movable:
            more = min(bound - holding[i], max(1, remaining * loads[i] // whole), rest)
            holding[i] = holding[i] + more
            rest = rest - more
    return np.array([bound] + holding)


def uneven(stream_key, number_of, total, bound, skew):
    if number_of == 2:
        one = jax.random.randint(stream_key, (), max(1, total - bound), min(bound, total - 1) + 1)
        return jnp.stack([one, total - one])
    lengths = jnp.asarray(length_profile(number_of, total, bound, skew), jnp.int32)
    pairs = (number_of - 1) // 2
    giver, sink = lengths[1:1 + 2 * pairs:2], lengths[2:2 + 2 * pairs:2]
    room = jnp.minimum(giver - 1, bound - sink)
    passed = jax.random.randint(jax.random.fold_in(stream_key, 1), (pairs,), 0, 1 << 20) % (room + 1)
    lengths = lengths.at[1:1 + 2 * pairs:2].set(giver - passed).at[2:2 + 2 * pairs:2].set(sink + passed)
    return lengths[jax.random.permutation(jax.random.fold_in(stream_key, 2), number_of)]


def bell_draw(key, shape, deviation, most, cuts=(), held_as=jnp.bfloat16):
    gain = steps_of(key, shape, cuts, -0.22, 0.18) if cuts else 1.0
    entries = jax.random.normal(key, shape, jnp.float32) * deviation * gain
    return jnp.minimum(jnp.maximum(entries, -most), most).astype(held_as)


def setup_inputs(seed: int = 0) -> dict:
    keys = jax.random.split(jax.random.key(seed), 7)
    return {
        "spins": draw_spins(jax.random.fold_in(keys[6], 71), 0),
        "energies": jnp.clip(-150.0 + 80.0 * jax.random.uniform(keys[1], (SLOTS_ALL,), jnp.float32) ** steps_of(keys[1], (SLOTS_ALL,), ((0, 16),), -0.2, 0.2), -150.0, -70.0).astype(jnp.bfloat16),
        "counts": uneven(keys[2], N_CHAIN, TOTAL, SLOTS_DEV, 2).astype(jnp.int32),
        "accepted": jax.vmap(lambda own: jax.random.permutation(own, SLOTS_DEV))(jax.random.split(keys[3], N_CHAIN)).reshape((N_CHAIN, SLOTS_DEV)).astype(jnp.int32),
        "hidden_bias": bell_draw(keys[4], (HIDDEN_SIZE,), 0.5, 3.0, ((0, 2),)),
        "weights": bell_draw(keys[5], (N_SITES, HIDDEN_SIZE), N_SITES ** -0.5, 0.375, ((1, 2),)),
    }


PRECISE = lax.Precision.HIGHEST
DIAG_SHIFT = 0.05
EPSILON = 1e-06

def activations(block_spins, hidden_bias, weights):
    preact = hidden_bias.astype(jnp.float32) + jnp.dot(block_spins, weights, preferred_element_type=jnp.float32)
    return jnp.tanh(preact).astype(jnp.bfloat16)

def combine(base_vec, extra_vec, factor):
    return tuple((first + factor * second for first, second in zip(base_vec, extra_vec)))

def inner(first_vec, second_vec):
    return jnp.sum(first_vec[0] * second_vec[0]) + jnp.sum(first_vec[1] * second_vec[1]) + jnp.sum(first_vec[2] * second_vec[2])

def reference(spins, energies, counts, accepted, hidden_bias, weights):
    sample_total = KEEP_DEV * N_CHAIN
    counts = counts.astype(jnp.int32)
    offsets = (jnp.cumsum(counts) - counts).astype(jnp.int32)
    global_rows = jnp.arange(sample_total, dtype=jnp.int32)
    owner_chain = (lax.optimization_barrier(jnp.sum((offsets[None, :] <= global_rows[:, None]).astype(jnp.int32), axis=1)) - 1).astype(jnp.int32)
    within = global_rows - offsets[owner_chain]
    local_slot = accepted[owner_chain, within].astype(jnp.int32)
    source_slot = owner_chain * SLOTS_DEV + local_slot
    samples = spins[source_slot]
    energy = energies[source_slot].astype(jnp.float32)
    centered = energy - jnp.mean(energy)
    block_rows = math.gcd(sample_total, 512)
    block_count = sample_total // block_rows
    blocks = samples.reshape(block_count, block_rows, N_SITES)

    def pull(row_weight):
        weight_blocks = row_weight.reshape(block_count, block_rows)

        def block_sums(running, block_item):
            block_spins, weight_rows = block_item
            hidden_acts = activations(block_spins, hidden_bias, weights).astype(jnp.float32)
            spins_float = block_spins.astype(jnp.float32)
            weighted = hidden_acts * weight_rows[:, None]
            grad_vis = jnp.dot(weight_rows, spins_float, precision=PRECISE)
            grad_hid = lax.optimization_barrier(jnp.sum(weighted, axis=0))
            grad_mat = jnp.dot(spins_float.T, weighted, precision=PRECISE)
            return ((running[0] + grad_vis, running[1] + grad_hid, running[2] + grad_mat), None)
        initial = (jnp.zeros((N_SITES,), jnp.float32), jnp.zeros((HIDDEN_SIZE,), jnp.float32), jnp.zeros((N_SITES, HIDDEN_SIZE), jnp.float32))
        results, unused = lax.scan(block_sums, initial, (blocks, weight_blocks))
        return tuple((member / sample_total for member in results))

    def forward(vector):
        vis_part, hid_part, mat_part = vector

        def block_values(running, block_spins):
            hidden_acts = activations(block_spins, hidden_bias, weights).astype(jnp.float32)
            spins_float = block_spins.astype(jnp.float32)
            mixture = jnp.dot(spins_float, mat_part, precision=PRECISE)
            values = lax.optimization_barrier(jnp.sum(mixture * hidden_acts, axis=1)) + jnp.dot(hidden_acts, hid_part, precision=PRECISE) + jnp.dot(spins_float, vis_part, precision=PRECISE)
            return (running, values)
        unused, results = lax.scan(block_values, jnp.zeros((), jnp.float32), blocks)
        row_values = results.reshape(sample_total)
        return row_values - jnp.mean(row_values)
    force = pull(centered)
    solution = tuple((jnp.zeros_like(member) for member in force))
    residual = force
    direction = force
    resid_sq = inner(residual, residual)
    for iteration in range(ITERS):
        image = combine(pull(forward(direction)), direction, DIAG_SHIFT)
        step_size = resid_sq / inner(direction, image)
        solution = combine(solution, direction, step_size)
        residual = combine(residual, image, -step_size)
        if iteration + 1 < ITERS:
            resid_next = inner(residual, residual)
            direction = combine(residual, direction, resid_next / resid_sq)
            resid_sq = resid_next
    param_total = N_SITES * HIDDEN_SIZE + HIDDEN_SIZE + N_SITES
    scale = 1.0 / jnp.sqrt(inner(solution, solution) / param_total + EPSILON)
    return (solution[0] * scale, solution[1] * scale, solution[2] * scale)
```

```python
import jax
import jax.numpy as jnp
from jax import lax
from jax.sharding import PartitionSpec as P

N_SITES = 256
HIDDEN_SIZE = 4096
KEEP_DEV = 768
ITERS = 3

DIAG_SHIFT = 0.05
EPSILON = 1e-06


def per_device(spins, energies, counts, accepted, hidden_bias, weights):
    chain_count = lax.axis_size("chain")
    slot_count, site_count = spins.shape
    hidden_part = weights.shape[1]
    visible_part = site_count // lax.axis_size("rep")
    matrix_rows = site_count // chain_count
    sample_total = KEEP_DEV * chain_count
    chain_pos = lax.axis_index("chain")
    rep_pos = lax.axis_index("rep")
    f32 = jnp.float32

    slots = jnp.arange(slot_count, dtype=jnp.int32)
    names = jnp.where(slots < counts[0], accepted[0], -1)
    live = jnp.sum((slots[:, None] == names[None, :]).astype(f32), axis=1)
    energy = energies.astype(f32) * live
    mean_energy = lax.psum(jnp.sum(energy), "chain") / sample_total
    centered = energy - mean_energy * live

    preact = hidden_bias.astype(f32) + jnp.dot(spins, weights, preferred_element_type=f32)
    acts = jnp.tanh(preact).astype(jnp.bfloat16)
    visible = lax.dynamic_slice_in_dim(spins, rep_pos * visible_part, visible_part, 1)

    def pull(row_weight):
        weighted = acts.astype(f32) * row_weight[:, None]
        mat = lax.dot_general(
            spins,
            weighted.astype(jnp.bfloat16),
            (((0,), (0,)), ((), ())),
            preferred_element_type=f32,
        )
        hid = jnp.sum(weighted, axis=0)
        vis = jnp.sum(visible.astype(f32) * row_weight[:, None], axis=0)
        mat = lax.psum((mat / sample_total).astype(jnp.bfloat16), "chain")
        vec = lax.psum(jnp.concatenate([hid, vis]) / sample_total, "chain")
        return (mat, vec[:hidden_part], vec[hidden_part:])

    def push(parts):
        mat, hid, vis = parts
        mixture = jnp.dot(spins, mat, preferred_element_type=f32) + hid
        row_values = jnp.sum(mixture * acts.astype(f32), axis=1)
        row_values = row_values + jnp.sum(visible.astype(f32) * vis, axis=1)
        return lax.psum(row_values, "rep") * live

    def sums(*pairs):
        return lax.psum(jnp.stack([jnp.sum(a * b) for a, b in pairs]), "chain")

    def mix(one, other, factor):
        return tuple(a + factor * b for a, b in zip(one, other))

    base = [pull(centered)]
    image_raw = push(base[0])
    total, = sums((image_raw, live))
    image0 = image_raw - live * (total / sample_total)
    unit = [jnp.array([1.0 if i == j else 0.0 for j in range(ITERS)], f32) for i in range(ITERS)]
    direction = (centered, image0, unit[0])
    residual = direction
    answer = tuple(jnp.zeros_like(a) for a in direction)
    resid_sq = None
    for iteration in range(ITERS):
        dd, dc, rc = sums((direction[1], direction[1]), (direction[1], direction[0]), (residual[1], residual[0]))
        if iteration == 0:
            resid_sq = rc
        step = resid_sq / (dd + DIAG_SHIFT * dc)
        answer = mix(answer, direction, step)
        if iteration + 1 == ITERS:
            break
        base.append(pull(direction[1]))
        raw = push(base[-1])
        total, = sums((raw, live))
        applied = (direction[1], raw - live * (total / sample_total), unit[iteration + 1])
        residual = mix(residual, mix(applied, direction, DIAG_SHIFT), -step)
        resid_next, = sums((residual[1], residual[0]))
        direction = mix(residual, direction, resid_next / resid_sq)
        resid_sq = resid_next
    norm_sq, = sums((answer[1], answer[0]))
    norm_sq = norm_sq / sample_total
    param_total = N_SITES * HIDDEN_SIZE + HIDDEN_SIZE + N_SITES
    scale = lax.rsqrt(norm_sq / param_total + EPSILON)
    pick = answer[2] * scale
    mat_out = 0.0
    hid_out = 0.0
    vis_out = 0.0
    for k, (mat, hid, vis) in enumerate(base):
        own = lax.dynamic_slice_in_dim(mat, chain_pos * matrix_rows, matrix_rows, 0)
        mat_out = mat_out + pick[k] * own.astype(f32)
        hid_out = hid_out + pick[k] * hid
        vis_out = vis_out + pick[k] * vis
    return (vis_out, hid_out, mat_out)


def solution(mesh):
    in_specs = (
        P("chain", None),
        P("chain"),
        P("chain"),
        P("chain", None),
        P("rep"),
        P(None, "rep"),
    )
    out_specs = (P("rep"), P("rep"), P("chain", "rep"))
    return jax.shard_map(
        per_device, mesh=mesh, in_specs=in_specs, out_specs=out_specs, check_vma=False
    )
```

```python
import functools

import jax
import jax.numpy as jnp
from jax import lax
from jax.experimental import pallas as pl
from jax.experimental.pallas import tpu as pltpu
from jax.sharding import PartitionSpec as P

N_SITES = 256
HIDDEN_SIZE = 4096
KEEP_DEV = 768
ITERS = 3

DIAG_SHIFT = 0.05
EPSILON = 1e-06
LANES = 128
MIN_ROWS = 16
MESH = pl.DeviceIdType.MESH
F32 = jnp.float32
BF16 = jnp.bfloat16


def to_row(column):
    return jnp.transpose(jnp.broadcast_to(column, (LANES, LANES)))[:1, :]


def to_column(row):
    return jnp.transpose(jnp.broadcast_to(row, (LANES, LANES)))[:, :1]


def total(values):
    return jnp.sum(values, axis=1, keepdims=True)


def kernel(
    n_chain, n_rep, s_ref, st_ref, wt_ref, bias_ref, energy_ref, live_ref,
    mat_ref, vec_ref, acts, acc, outbox, inbox, pulled, vecs, vec_in, rowsum, rows, gathered,
    mat_send, mat_recv, back_send, back_recv, vec_send, vec_recv, row_send, row_recv,
    tell_send, tell_recv,
):
    slots, sites = s_ref.shape
    hidden = wt_ref.shape[0]
    visible = sites // n_rep
    sample_total = float(KEEP_DEV * n_chain)
    bits = n_chain.bit_length() - 1
    tile = min(256, hidden // 2)
    chunks = tile // LANES
    vis_row = hidden // LANES
    me = lax.axis_index("chain")
    rep = lax.axis_index("rep")
    lane = lax.broadcasted_iota(jnp.int32, (1, LANES), 1)

    barrier = pltpu.get_barrier_semaphore()

    @pl.loop(1, n_chain)
    def _(k):
        pl.semaphore_signal(
            barrier, inc=1, device_id={"chain": lax.rem(me + k, n_chain)}, device_id_type=MESH
        )

    for k in range(1, n_rep):
        pl.semaphore_signal(
            barrier, inc=1, device_id={"rep": lax.rem(rep + k, n_rep)}, device_id_type=MESH
        )
    pl.semaphore_wait(barrier, n_chain - 1 + n_rep - 1)

    def tell_copy(sync, source, target):
        return pltpu.make_async_remote_copy(
            src_ref=gathered.at[sync, source],
            dst_ref=gathered.at[sync, source],
            send_sem=tell_send.at[sync, target],
            recv_sem=tell_recv.at[sync, source],
            device_id={"chain": target},
            device_id_type=MESH,
        )

    def tell(sync, values):
        packed = jnp.zeros((1, LANES), F32)
        for j, value in enumerate(values):
            packed = jnp.where(lane == j, value, packed)
        weight = jnp.broadcast_to(values[0], (1, LANES))
        middle = jnp.broadcast_to(values[1], (1, LANES))
        blank = jnp.zeros((5, LANES), F32)
        gathered[sync, me] = jnp.concatenate([packed, weight, middle, blank], axis=0)

        @pl.loop(1, n_chain)
        def _(k):
            tell_copy(sync, me, lax.rem(me + k, n_chain)).start()

    def hear(sync, count):
        @pl.loop(1, n_chain)
        def _(k):
            tell_copy(sync, lax.rem(me + k, n_chain), lax.rem(me + k, n_chain)).wait_recv()

        @pl.loop(1, n_chain)
        def _(k):
            tell_copy(sync, me, lax.rem(me + k, n_chain)).wait_send()

        everyone = [gathered[sync, j] for j in range(n_chain)]
        packed = everyone[0][0:1]
        weighted = everyone[0][1:2] * everyone[0][2:3]
        for one in everyone[1:]:
            packed = packed + one[0:1]
            weighted = weighted + one[1:2] * one[2:3]
        mean = weighted / sample_total
        spread = jnp.zeros((1, LANES), F32)
        for one in everyone:
            spread = spread + one[1:2] * (one[2:3] - mean) * (one[2:3] - mean)
        found = [total(jnp.where(lane == j, packed, 0.0)) for j in range(count)]
        return mean[:, :1], spread[:, :1], found

    vecs[...] = jnp.zeros_like(vecs)
    live = live_ref[...]
    own_count = total(live)
    energy = energy_ref[...]
    tell(0, [own_count, total(energy * live) / own_count])

    @pl.loop(0, hidden // tile)
    def _(i):
        part = pl.ds(pl.multiple_of(i * tile, tile), tile)
        preact = jnp.dot(wt_ref[part, :], st_ref[...], preferred_element_type=F32)
        bias = [to_column(bias_ref[pl.ds(i * chunks + r, 1), :]) for r in range(chunks)]
        acts[part, :] = jnp.tanh(preact + jnp.concatenate(bias, axis=0)).astype(BF16)

    mean_energy, _, _ = hear(0, 0)
    centered = (energy - mean_energy) * live

    own_visible = pl.ds(pl.multiple_of(rep * visible, visible), visible)

    def pull_tiles(k, first, count, row_weight):
        @pl.loop(0, count)
        def _(i):
            begin = first + i * tile
            part = pl.ds(pl.multiple_of(begin, tile), tile)
            weighted = acts[part, :].astype(F32) * row_weight
            sums = jnp.sum(weighted, axis=1, keepdims=True)
            for r in range(chunks):
                row = to_row(sums[r * LANES : (r + 1) * LANES])
                vecs[k, pl.ds(begin // LANES + r, 1), :] = row
            acc[part, :] = jnp.dot(
                weighted.astype(BF16), s_ref[...], preferred_element_type=F32
            )

    def peer(b):
        digit = lax.rem(me // (2**b), 2)
        return digit, me + (1 - 2 * digit) * (2**b)

    def push_tiles(k, first, count):
        @pl.loop(0, count)
        def _(i):
            begin = first + i * tile
            part = pl.ds(pl.multiple_of(begin, tile), tile)
            mixture = jnp.dot(pulled[k, part, :], st_ref[...], preferred_element_type=F32)
            shift = [to_column(vecs[k, pl.ds(begin // LANES + r, 1), :]) for r in range(chunks)]
            mixture = mixture + jnp.concatenate(shift, axis=0)
            product = mixture * acts[part, :].astype(F32)
            rowsum[...] += jnp.sum(product.reshape(tile // 8, 8, slots), axis=0)

    def apply(k, row_weight):
        row_weight = row_weight / sample_total
        sums = jnp.sum(st_ref[own_visible, :].astype(F32) * row_weight, axis=1, keepdims=True)
        if visible < LANES:
            sums = jnp.concatenate([sums, jnp.zeros((LANES - visible, 1), F32)], axis=0)
        vecs[k, vis_row : vis_row + 1, :] = to_row(sums)

        start, size, place = 0, hidden, 0
        steps = []
        for b in range(bits):
            digit, partner = peer(b)
            split = size // 2 >= MIN_ROWS
            moved = size // 2 if split else size
            away = start + (1 - digit) * moved if split else start
            keep = start + digit * moved if split else start
            away = pl.multiple_of(away, moved)
            keep = pl.multiple_of(keep, moved)
            if b == 0:
                pull_tiles(k, away, moved // tile, row_weight)
            outbox[pl.ds(place, moved), :] = acc[pl.ds(away, moved), :].astype(BF16)
            send = pltpu.make_async_remote_copy(
                src_ref=outbox.at[pl.ds(place, moved)],
                dst_ref=inbox.at[pl.ds(place, moved)],
                send_sem=mat_send.at[k, b],
                recv_sem=mat_recv.at[k, b],
                device_id={"chain": partner},
                device_id_type=MESH,
            )
            send.start()
            if b == 0:
                pull_tiles(k, keep, moved // tile, row_weight)
            spread = pltpu.make_async_remote_copy(
                src_ref=vecs.at[k],
                dst_ref=vec_in.at[k, b],
                send_sem=vec_send.at[k, b],
                recv_sem=vec_recv.at[k, b],
                device_id={"chain": partner},
                device_id_type=MESH,
            )
            spread.start()
            send.wait()
            own = acc[pl.ds(keep, moved), :]
            if not split:
                own = own.astype(BF16).astype(F32)
            acc[pl.ds(keep, moved), :] = own + inbox[pl.ds(place, moved), :].astype(F32)
            spread.wait()
            vecs[k] = vecs[k] + vec_in[k, b]
            place += moved
            start, size = keep, moved
            steps.append((b, partner, split, keep, moved))
        pulled[k, pl.ds(start, size), :] = acc[pl.ds(start, size), :].astype(BF16)
        rowsum[...] = jnp.zeros_like(rowsum)
        for b, partner, split, keep, moved in reversed(steps):
            if not split:
                continue
            part = pl.ds(pl.multiple_of(keep, moved), moved)
            send = pltpu.make_async_remote_copy(
                src_ref=pulled.at[k, part],
                dst_ref=pulled.at[k, part],
                send_sem=back_send.at[k, b],
                recv_sem=back_recv.at[k, b],
                device_id={"chain": partner},
                device_id_type=MESH,
            )
            send.start()
            if b == 0:
                push_tiles(k, keep, moved // tile)
            send.wait()
            if b == 0:
                push_tiles(k, hidden - moved - keep, moved // tile)
        seen = jnp.sum(rowsum[...], axis=0, keepdims=True)
        effect = to_column(vecs[k, vis_row : vis_row + 1, :])[:visible]
        seen = seen + jnp.sum(st_ref[own_visible, :].astype(F32) * effect, axis=0, keepdims=True)
        rows[k, rep, 0:1, :] = seen

        def row_copy(source, target):
            return pltpu.make_async_remote_copy(
                src_ref=rows.at[k, source, pl.ds(0, 1)],
                dst_ref=rows.at[k, source, pl.ds(0, 1)],
                send_sem=row_send.at[k, target],
                recv_sem=row_recv.at[k, source],
                device_id={"rep": target},
                device_id_type=MESH,
            )

        others = [lax.rem(rep + d, n_rep) for d in range(1, n_rep)]
        for other in others:
            row_copy(rep, other).start()
        for other in others:
            row_copy(other, other).wait_recv()
        for other in others:
            row_copy(rep, other).wait_send()
        whole = rows[k, 0, 0:1, :]
        for j in range(1, n_rep):
            whole = whole + rows[k, j, 0:1, :]
        return whole * live

    raw = apply(0, centered)
    middle = total(raw) / own_count
    local = (raw - middle) * live
    tell(1, [own_count, middle, total(local * local), total(raw * centered)])
    mean, spread, found = hear(1, 4)
    image = (raw - mean) * live
    dir_dir = found[2] + spread
    dir_wgt = found[3]
    resid_sq = dir_wgt
    dir_w, dir_o, dir_c = centered, image, [1.0, 0.0, 0.0]
    res_w, res_o, res_c = centered, image, [1.0, 0.0, 0.0]
    step = resid_sq / (dir_dir + DIAG_SHIFT * dir_wgt)
    ans_w, ans_o = step * dir_w, step * dir_o
    ans_c = [step * x for x in dir_c]
    norm = None
    for i in range(1, ITERS):
        raw = apply(i, dir_o)
        unit = [1.0 if j == i else 0.0 for j in range(ITERS)]
        res_w = res_w - step * (dir_o + DIAG_SHIFT * dir_w)
        res_c = [r - step * (u + DIAG_SHIFT * d) for r, u, d in zip(res_c, unit, dir_c)]
        fresh = res_o - step * (raw + DIAG_SHIFT * dir_o)
        middle = total(fresh * live) / own_count
        local = (fresh - middle) * live
        tell(i + 1, [
            own_count, middle, total(local * local), total(fresh * dir_o), total(fresh * res_w),
            total(fresh * dir_w), total(dir_o * res_w), total(fresh * ans_w),
            total(dir_o * ans_w), total(ans_o * ans_w),
        ])
        mean, spread, found = hear(i + 1, 10)
        res_o = (fresh - mean) * live
        _, _, res_res, res_dir, resid_next, res_dirw, dir_resw, res_ans, dir_ans, ans_ans = found
        res_res = res_res + spread
        ratio = resid_next / resid_sq
        new_dir = res_res + 2.0 * ratio * res_dir + ratio * ratio * dir_dir
        new_wgt = resid_next + ratio * (res_dirw + dir_resw) + ratio * ratio * dir_wgt
        mixed = res_ans + ratio * dir_ans
        dir_w = res_w + ratio * dir_w
        dir_o = res_o + ratio * dir_o
        dir_c = [r + ratio * d for r, d in zip(res_c, dir_c)]
        dir_dir, dir_wgt, resid_sq = new_dir, new_wgt, resid_next
        step = resid_sq / (dir_dir + DIAG_SHIFT * dir_wgt)
        norm = (ans_ans + 2.0 * step * mixed + step * step * dir_wgt) / sample_total
        ans_w, ans_o = ans_w + step * dir_w, ans_o + step * dir_o
        ans_c = [a + step * d for a, d in zip(ans_c, dir_c)]
    params = N_SITES * HIDDEN_SIZE + HIDDEN_SIZE + N_SITES
    scale = lax.rsqrt(norm / params + EPSILON)
    own_rows = mat_ref.shape[0]
    picks = lax.broadcasted_iota(jnp.int32, (MIN_ROWS, sites), 0) + me * own_rows
    picks = (picks == lax.broadcasted_iota(jnp.int32, (MIN_ROWS, sites), 1)).astype(BF16)
    for i in range(hidden // tile):
        part = slice(i * tile, (i + 1) * tile)
        out = 0.0
        for k in range(ITERS):
            piece = lax.dot_general(
                picks, pulled[k, part, :], (((1,), (1,)), ((), ())), preferred_element_type=F32
            )
            out = out + (ans_c[k] * scale) * piece
        mat_ref[:, part] = out[:own_rows]
    vec = 0.0
    for k in range(ITERS):
        vec = vec + (ans_c[k] * scale) * vecs[k]
    vec_ref[...] = vec


def per_device(spins, energies, counts, accepted, hidden_bias, weights):
    n_chain = lax.axis_size("chain")
    n_rep = lax.axis_size("rep")
    slots, sites = spins.shape
    hidden = weights.shape[1]
    visible = sites // n_rep
    bits = n_chain.bit_length() - 1
    vec_rows = -(-(hidden // LANES + 1) // 8) * 8
    order = jnp.arange(slots, dtype=jnp.int32)
    names = jnp.where(order < counts[0], accepted[0], -1)
    live = jnp.any(order[:, None] == names[None, :], axis=1).astype(F32)
    vmem = pl.BlockSpec(memory_space=pltpu.VMEM)
    dma = pltpu.SemaphoreType.DMA
    mat, vec = pl.pallas_call(
        functools.partial(kernel, n_chain, n_rep),
        out_shape=(
            jax.ShapeDtypeStruct((sites // n_chain, hidden), F32),
            jax.ShapeDtypeStruct((vec_rows, LANES), F32),
        ),
        in_specs=[vmem] * 6,
        out_specs=(vmem, vmem),
        scratch_shapes=[
            pltpu.VMEM((hidden, slots), BF16),
            pltpu.VMEM((hidden, sites), F32),
            pltpu.VMEM((hidden + MIN_ROWS * bits, sites), BF16),
            pltpu.VMEM((hidden + MIN_ROWS * bits, sites), BF16),
            pltpu.VMEM((ITERS, hidden, sites), BF16),
            pltpu.VMEM((ITERS, vec_rows, LANES), F32),
            pltpu.VMEM((ITERS, bits, vec_rows, LANES), F32),
            pltpu.VMEM((8, slots), F32),
            pltpu.VMEM((ITERS, n_rep, 8, slots), F32),
            pltpu.VMEM((ITERS + 1, n_chain, 8, LANES), F32),
            dma((ITERS, bits)),
            dma((ITERS, bits)),
            dma((ITERS, bits)),
            dma((ITERS, bits)),
            dma((ITERS, bits)),
            dma((ITERS, bits)),
            dma((ITERS, n_rep)),
            dma((ITERS, n_rep)),
            dma((ITERS + 1, n_chain)),
            dma((ITERS + 1, n_chain)),
        ],
        compiler_params=pltpu.CompilerParams(
            collective_id=0, has_side_effects=True, vmem_limit_bytes=60 * 1024 * 1024
        ),
    )(
        spins,
        spins.T,
        weights.T,
        hidden_bias.astype(F32).reshape(hidden // LANES, LANES),
        energies.astype(F32)[None],
        live[None],
    )
    flat = vec.reshape(-1)
    return flat[hidden : hidden + visible], flat[:hidden], mat


def solution(mesh):
    in_specs = (
        P("chain", None),
        P("chain"),
        P("chain"),
        P("chain", None),
        P("rep"),
        P(None, "rep"),
    )
    out_specs = (P("rep"), P("rep"), P("chain", "rep"))
    return jax.shard_map(
        per_device, mesh=mesh, in_specs=in_specs, out_specs=out_specs, check_vma=False
    )
```

```python
import functools

import jax
import jax.numpy as jnp
from jax import lax
from jax.experimental import pallas as pl
from jax.experimental.pallas import tpu as pltpu
from jax.sharding import PartitionSpec as P

N_SITES = 256
HIDDEN_SIZE = 4096
KEEP_DEV = 768
ITERS = 3

DIAG_SHIFT = 0.05
EPSILON = 1e-06
LANES = 128
MAX_STRANDS = 4
MIN_ROWS = 16
MESH = pl.DeviceIdType.MESH
F32 = jnp.float32
BF16 = jnp.bfloat16


def to_row(column):
    return jnp.transpose(jnp.broadcast_to(column, (LANES, LANES)))[:1, :]


def to_column(row):
    return jnp.transpose(jnp.broadcast_to(row, (LANES, LANES)))[:, :1]


def bit_order(strand, bits):
    rest = list(range(1, bits))
    turn = strand % len(rest)
    return [0] + rest[turn:] + rest[:turn]


def total(values):
    return jnp.sum(values, axis=1, keepdims=True)


def kernel(
    n_chain, n_rep, s_ref, st_ref, wt_ref, bias_ref, energy_ref, live_ref,
    mat_ref, vec_ref, acts, acc, outbox, inbox, pulled, vecs, vec_in, rowsum, rows, gathered,
    mat_send, mat_recv, back_send, back_recv, vec_send, vec_recv, row_send, row_recv,
    tell_send, tell_recv,
):
    slots, sites = s_ref.shape
    hidden = wt_ref.shape[0]
    visible = sites // n_rep
    sample_total = float(KEEP_DEV * n_chain)
    bits = n_chain.bit_length() - 1
    strands = min(MAX_STRANDS, hidden // 256)
    tile = min(256, hidden // (2 * strands))
    chunks = tile // LANES
    vis_row = hidden // LANES
    me = lax.axis_index("chain")
    rep = lax.axis_index("rep")
    lane = lax.broadcasted_iota(jnp.int32, (1, LANES), 1)

    barrier = pltpu.get_barrier_semaphore()

    @pl.loop(1, n_chain)
    def _(k):
        pl.semaphore_signal(
            barrier, inc=1, device_id={"chain": lax.rem(me + k, n_chain)}, device_id_type=MESH
        )

    for k in range(1, n_rep):
        pl.semaphore_signal(
            barrier, inc=1, device_id={"rep": lax.rem(rep + k, n_rep)}, device_id_type=MESH
        )
    pl.semaphore_wait(barrier, n_chain - 1 + n_rep - 1)

    def tell_copy(sync, source, target):
        return pltpu.make_async_remote_copy(
            src_ref=gathered.at[sync, source],
            dst_ref=gathered.at[sync, source],
            send_sem=tell_send.at[sync, target],
            recv_sem=tell_recv.at[sync, source],
            device_id={"chain": target},
            device_id_type=MESH,
        )

    def tell(sync, values):
        packed = jnp.zeros((1, LANES), F32)
        for j, value in enumerate(values):
            packed = jnp.where(lane == j, value, packed)
        weight = jnp.broadcast_to(values[0], (1, LANES))
        middle = jnp.broadcast_to(values[1], (1, LANES))
        blank = jnp.zeros((5, LANES), F32)
        gathered[sync, me] = jnp.concatenate([packed, weight, middle, blank], axis=0)

        @pl.loop(1, n_chain)
        def _(k):
            tell_copy(sync, me, lax.rem(me + k, n_chain)).start()

    def hear(sync, count):
        @pl.loop(1, n_chain)
        def _(k):
            tell_copy(sync, lax.rem(me + k, n_chain), lax.rem(me + k, n_chain)).wait_recv()

        @pl.loop(1, n_chain)
        def _(k):
            tell_copy(sync, me, lax.rem(me + k, n_chain)).wait_send()

        everyone = [gathered[sync, j] for j in range(n_chain)]
        packed = everyone[0][0:1]
        weighted = everyone[0][1:2] * everyone[0][2:3]
        for one in everyone[1:]:
            packed = packed + one[0:1]
            weighted = weighted + one[1:2] * one[2:3]
        mean = weighted / sample_total
        spread = jnp.zeros((1, LANES), F32)
        for one in everyone:
            spread = spread + one[1:2] * (one[2:3] - mean) * (one[2:3] - mean)
        found = [total(jnp.where(lane == j, packed, 0.0)) for j in range(count)]
        return mean[:, :1], spread[:, :1], found

    vecs[...] = jnp.zeros_like(vecs)
    live = live_ref[...]
    own_count = total(live)
    energy = energy_ref[...]
    tell(0, [own_count, total(energy * live) / own_count])

    @pl.loop(0, hidden // tile)
    def _(i):
        part = pl.ds(pl.multiple_of(i * tile, tile), tile)
        preact = jnp.dot(wt_ref[part, :], st_ref[...], preferred_element_type=F32)
        bias = [to_column(bias_ref[pl.ds(i * chunks + r, 1), :]) for r in range(chunks)]
        acts[part, :] = jnp.tanh(preact + jnp.concatenate(bias, axis=0)).astype(BF16)

    mean_energy, _, _ = hear(0, 0)
    centered = (energy - mean_energy) * live

    own_visible = pl.ds(pl.multiple_of(rep * visible, visible), visible)

    def pull_tiles(k, first, count, row_weight):
        @pl.loop(0, count)
        def _(i):
            begin = first + i * tile
            part = pl.ds(pl.multiple_of(begin, tile), tile)
            weighted = acts[part, :].astype(F32) * row_weight
            sums = jnp.sum(weighted, axis=1, keepdims=True)
            for r in range(chunks):
                row = to_row(sums[r * LANES : (r + 1) * LANES])
                vecs[k, pl.ds(begin // LANES + r, 1), :] = row
            acc[part, :] = jnp.dot(
                weighted.astype(BF16), s_ref[...], preferred_element_type=F32
            )

    def peer(b):
        digit = lax.rem(me // (2**b), 2)
        return digit, me + (1 - 2 * digit) * (2**b)

    def push_tiles(k, first, count):
        @pl.loop(0, count)
        def _(i):
            begin = first + i * tile
            part = pl.ds(pl.multiple_of(begin, tile), tile)
            mixture = jnp.dot(pulled[k, part, :], st_ref[...], preferred_element_type=F32)
            shift = [to_column(vecs[k, pl.ds(begin // LANES + r, 1), :]) for r in range(chunks)]
            mixture = mixture + jnp.concatenate(shift, axis=0)
            product = mixture * acts[part, :].astype(F32)
            rowsum[...] += jnp.sum(product.reshape(tile // 8, 8, slots), axis=0)

    def apply(k, row_weight):
        row_weight = row_weight / sample_total
        sums = jnp.sum(st_ref[own_visible, :].astype(F32) * row_weight, axis=1, keepdims=True)
        if visible < LANES:
            sums = jnp.concatenate([sums, jnp.zeros((LANES - visible, 1), F32)], axis=0)
        vecs[k, vis_row : vis_row + 1, :] = to_row(sums)

        rowsum[...] = jnp.zeros_like(rowsum)

        def mat_copy(source, target, sends, recvs, slot, partner):
            return pltpu.make_async_remote_copy(
                src_ref=source,
                dst_ref=target,
                send_sem=sends.at[k, slot],
                recv_sem=recvs.at[k, slot],
                device_id={"chain": partner},
                device_id_type=MESH,
            )

        def strand(c, order):
            size = hidden // strands
            start, place = c * size, c * (size + MIN_ROWS * bits)
            steps = []
            for b in order:
                digit, partner = peer(b)
                split = size // 2 >= MIN_ROWS
                moved = size // 2 if split else size
                away = start + (1 - digit) * moved if split else start
                keep = start + digit * moved if split else start
                away = pl.multiple_of(away, moved)
                keep = pl.multiple_of(keep, moved)
                if b == order[0]:
                    pull_tiles(k, away, moved // tile, row_weight)
                outbox[pl.ds(place, moved), :] = acc[pl.ds(away, moved), :].astype(BF16)
                box = pl.ds(place, moved)
                send = mat_copy(
                    outbox.at[box], inbox.at[box], mat_send, mat_recv, c * bits + b, partner
                )
                send.start()
                yield
                if b == order[0]:
                    pull_tiles(k, keep, moved // tile, row_weight)
                send.wait()
                own = acc[pl.ds(keep, moved), :]
                if not split:
                    own = own.astype(BF16).astype(F32)
                acc[pl.ds(keep, moved), :] = own + inbox[box, :].astype(F32)
                place += moved
                start, size = keep, moved
                steps.append((b, partner, split, keep, moved))
            pulled[k, pl.ds(start, size), :] = acc[pl.ds(start, size), :].astype(BF16)
            for b, partner, split, keep, moved in reversed(steps):
                if not split:
                    continue
                part = pulled.at[k, pl.ds(pl.multiple_of(keep, moved), moved)]
                send = mat_copy(part, part, back_send, back_recv, c * bits + b, partner)
                send.start()
                yield
                if b == order[0]:
                    push_tiles(k, keep, moved // tile)
                    yield
                send.wait()
                if b == order[0]:
                    other = 2 * c * (hidden // strands) + hidden // strands - moved - keep
                    push_tiles(k, other, moved // tile)

        def vec_strand():
            yield
            for b in range(bits):
                spread = pltpu.make_async_remote_copy(
                    src_ref=vecs.at[k],
                    dst_ref=vec_in.at[k, b],
                    send_sem=vec_send.at[k, b],
                    recv_sem=vec_recv.at[k, b],
                    device_id={"chain": peer(b)[1]},
                    device_id_type=MESH,
                )
                spread.start()
                yield
                spread.wait()
                vecs[k] = vecs[k] + vec_in[k, b]

        active = [strand(c, bit_order(c, bits)) for c in range(strands)] + [vec_strand()]
        while active:
            active = [one for one in active if next(one, active) is not active]
        seen = jnp.sum(rowsum[...], axis=0, keepdims=True)
        effect = to_column(vecs[k, vis_row : vis_row + 1, :])[:visible]
        seen = seen + jnp.sum(st_ref[own_visible, :].astype(F32) * effect, axis=0, keepdims=True)
        rows[k, rep, 0:1, :] = seen

        def row_copy(source, target):
            return pltpu.make_async_remote_copy(
                src_ref=rows.at[k, source, pl.ds(0, 1)],
                dst_ref=rows.at[k, source, pl.ds(0, 1)],
                send_sem=row_send.at[k, target],
                recv_sem=row_recv.at[k, source],
                device_id={"rep": target},
                device_id_type=MESH,
            )

        others = [lax.rem(rep + d, n_rep) for d in range(1, n_rep)]
        for other in others:
            row_copy(rep, other).start()
        for other in others:
            row_copy(other, other).wait_recv()
        for other in others:
            row_copy(rep, other).wait_send()
        whole = rows[k, 0, 0:1, :]
        for j in range(1, n_rep):
            whole = whole + rows[k, j, 0:1, :]
        return whole * live

    raw = apply(0, centered)
    middle = total(raw) / own_count
    local = (raw - middle) * live
    tell(1, [own_count, middle, total(local * local), total(raw * centered)])
    mean, spread, found = hear(1, 4)
    image = (raw - mean) * live
    dir_dir = found[2] + spread
    dir_wgt = found[3]
    resid_sq = dir_wgt
    dir_w, dir_o, dir_c = centered, image, [1.0, 0.0, 0.0]
    res_w, res_o, res_c = centered, image, [1.0, 0.0, 0.0]
    step = resid_sq / (dir_dir + DIAG_SHIFT * dir_wgt)
    ans_w, ans_o = step * dir_w, step * dir_o
    ans_c = [step * x for x in dir_c]
    norm = None
    for i in range(1, ITERS):
        raw = apply(i, dir_o)
        unit = [1.0 if j == i else 0.0 for j in range(ITERS)]
        res_w = res_w - step * (dir_o + DIAG_SHIFT * dir_w)
        res_c = [r - step * (u + DIAG_SHIFT * d) for r, u, d in zip(res_c, unit, dir_c)]
        fresh = res_o - step * (raw + DIAG_SHIFT * dir_o)
        middle = total(fresh * live) / own_count
        local = (fresh - middle) * live
        tell(i + 1, [
            own_count, middle, total(local * local), total(fresh * dir_o), total(fresh * res_w),
            total(fresh * dir_w), total(dir_o * res_w), total(fresh * ans_w),
            total(dir_o * ans_w), total(ans_o * ans_w),
        ])
        mean, spread, found = hear(i + 1, 10)
        res_o = (fresh - mean) * live
        _, _, res_res, res_dir, resid_next, res_dirw, dir_resw, res_ans, dir_ans, ans_ans = found
        res_res = res_res + spread
        ratio = resid_next / resid_sq
        new_dir = res_res + 2.0 * ratio * res_dir + ratio * ratio * dir_dir
        new_wgt = resid_next + ratio * (res_dirw + dir_resw) + ratio * ratio * dir_wgt
        mixed = res_ans + ratio * dir_ans
        dir_w = res_w + ratio * dir_w
        dir_o = res_o + ratio * dir_o
        dir_c = [r + ratio * d for r, d in zip(res_c, dir_c)]
        dir_dir, dir_wgt, resid_sq = new_dir, new_wgt, resid_next
        step = resid_sq / (dir_dir + DIAG_SHIFT * dir_wgt)
        norm = (ans_ans + 2.0 * step * mixed + step * step * dir_wgt) / sample_total
        ans_w, ans_o = ans_w + step * dir_w, ans_o + step * dir_o
        ans_c = [a + step * d for a, d in zip(ans_c, dir_c)]
    params = N_SITES * HIDDEN_SIZE + HIDDEN_SIZE + N_SITES
    scale = lax.rsqrt(norm / params + EPSILON)
    own_rows = mat_ref.shape[0]
    picks = lax.broadcasted_iota(jnp.int32, (MIN_ROWS, sites), 0) + me * own_rows
    picks = (picks == lax.broadcasted_iota(jnp.int32, (MIN_ROWS, sites), 1)).astype(BF16)
    for i in range(hidden // tile):
        part = slice(i * tile, (i + 1) * tile)
        out = 0.0
        for k in range(ITERS):
            piece = lax.dot_general(
                picks, pulled[k, part, :], (((1,), (1,)), ((), ())), preferred_element_type=F32
            )
            out = out + (ans_c[k] * scale) * piece
        mat_ref[:, part] = out[:own_rows]
    vec = 0.0
    for k in range(ITERS):
        vec = vec + (ans_c[k] * scale) * vecs[k]
    vec_ref[...] = vec


def per_device(spins, energies, counts, accepted, hidden_bias, weights):
    n_chain = lax.axis_size("chain")
    n_rep = lax.axis_size("rep")
    slots, sites = spins.shape
    hidden = weights.shape[1]
    visible = sites // n_rep
    bits = n_chain.bit_length() - 1
    strands = min(MAX_STRANDS, hidden // 256)
    vec_rows = -(-(hidden // LANES + 1) // 8) * 8
    order = jnp.arange(slots, dtype=jnp.int32)
    names = jnp.where(order < counts[0], accepted[0], -1)
    live = jnp.any(order[:, None] == names[None, :], axis=1).astype(F32)
    vmem = pl.BlockSpec(memory_space=pltpu.VMEM)
    dma = pltpu.SemaphoreType.DMA
    mat, vec = pl.pallas_call(
        functools.partial(kernel, n_chain, n_rep),
        out_shape=(
            jax.ShapeDtypeStruct((sites // n_chain, hidden), F32),
            jax.ShapeDtypeStruct((vec_rows, LANES), F32),
        ),
        in_specs=[vmem] * 6,
        out_specs=(vmem, vmem),
        scratch_shapes=[
            pltpu.VMEM((hidden, slots), BF16),
            pltpu.VMEM((hidden, sites), F32),
            pltpu.VMEM((hidden + strands * MIN_ROWS * bits, sites), BF16),
            pltpu.VMEM((hidden + strands * MIN_ROWS * bits, sites), BF16),
            pltpu.VMEM((ITERS, hidden, sites), BF16),
            pltpu.VMEM((ITERS, vec_rows, LANES), F32),
            pltpu.VMEM((ITERS, bits, vec_rows, LANES), F32),
            pltpu.VMEM((8, slots), F32),
            pltpu.VMEM((ITERS, n_rep, 8, slots), F32),
            pltpu.VMEM((ITERS + 1, n_chain, 8, LANES), F32),
            dma((ITERS, strands * bits)),
            dma((ITERS, strands * bits)),
            dma((ITERS, strands * bits)),
            dma((ITERS, strands * bits)),
            dma((ITERS, bits)),
            dma((ITERS, bits)),
            dma((ITERS, n_rep)),
            dma((ITERS, n_rep)),
            dma((ITERS + 1, n_chain)),
            dma((ITERS + 1, n_chain)),
        ],
        compiler_params=pltpu.CompilerParams(
            collective_id=0, has_side_effects=True, vmem_limit_bytes=60 * 1024 * 1024
        ),
    )(
        spins,
        spins.T,
        weights.T,
        hidden_bias.astype(F32).reshape(hidden // LANES, LANES),
        energies.astype(F32)[None],
        live[None],
    )
    flat = vec.reshape(-1)
    return flat[hidden : hidden + visible], flat[:hidden], mat


def solution(mesh):
    in_specs = (
        P("chain", None),
        P("chain"),
        P("chain"),
        P("chain", None),
        P("rep"),
        P(None, "rep"),
    )
    out_specs = (P("rep"), P("rep"), P("chain", "rep"))
    return jax.shard_map(
        per_device, mesh=mesh, in_specs=in_specs, out_specs=out_specs, check_vma=False
    )
```
